32 devices in a mesh: pipe: 4 (over z), ctx: 4 (over y, x), exp: 2 (over core).
Axes of the slice: x: 2, y: 2, z: 4, core: 2. Of those that a mesh axis runs over, the one named last changes fastest.
Arguments:
- mix_input: bfloat16 [4, 512, 8192], P('pipe', 'ctx', 'exp'), may hold values from -6 to 6
- state_write: bfloat16 [4, 512, 64], P('pipe', 'ctx'), may hold values from -2.5 to 2.5
- state_read: bfloat16 [4, 512, 64], P('pipe', 'ctx'), may hold values from -2.5 to 2.5
- log_decay: float32 [4, 512, 128], P('pipe', 'ctx', 'exp'), may hold values from -1 to 0
- skip_gain: float32 [128], P('exp'), may hold values from 0.5 to 1.5
- query_rows: bfloat16 [4, 512, 8192], P('pipe', 'ctx', 'exp'), may hold values from -39.774756 to 39.774756
- key_rows: bfloat16 [4, 512, 1024], P('pipe', 'ctx', 'exp'), may hold values from -8 to 8
- value_rows: bfloat16 [4, 512, 1024], P('pipe', 'ctx', 'exp'), may hold values from -6 to 6
- incoming: bfloat16 [512, 8192], P('ctx', 'exp'), may hold values from -6 to 6
- norm_gain: float32 [8192], P('exp'), may hold values from 0.5 to 1.5
Outputs:
- mamba_out: bfloat16 [4, 512, 8192], P('pipe', 'ctx', 'exp')
- block_out: bfloat16 [4, 512, 8192], P('pipe', 'ctx', 'exp')
The draws below stay inside these ranges and needn't reach their ends.
All inputs are finite; a program needn't handle non-finite values.
Results may differ from the reference program's by a relative error of at most 0.013.
Values may be sent and summed in bfloat16 or wider, within the bound.
A program may use at most 128 MiB of HBM per device.

```python
import jax
import jax.numpy as jnp
from jax import lax

D = 8192
HEADS = 64
KV_HEADS = 8
HEAD_DIM = 128
MIXER_HEADS = 128
SSD_DIM = 64
NSTATE = 64
TOK_DEV = 128
SEQUENCE_LENGTH = 512
RELAY_SEGMENTS = 4


def query_key_pair(key):
    base_key = jax.random.fold_in(key, 11)
    context_pieces = jax.random.split(base_key, 2)
    query_shape = (RELAY_SEGMENTS, SEQUENCE_LENGTH, HEADS * HEAD_DIM)
    key_shape = (RELAY_SEGMENTS, SEQUENCE_LENGTH, KV_HEADS * HEAD_DIM)
    queries = jax.random.normal(context_pieces[0], query_shape, jnp.float32)
    key_table = jax.random.normal(context_pieces[1], key_shape, jnp.float32)
    return (queries, key_table)


def draw_query_rows(key, part):
    return query_key_pair(key)[0].astype(jnp.bfloat16)


def draw_key_rows(key, part):
    return query_key_pair(key)[1].astype(jnp.bfloat16)


def decay_plan(key):
    base_key = jax.random.fold_in(key, 23)
    context_pieces = jax.random.split(base_key, 7)
    fast_share = 0.2
    middle_share = 0.3
    head_shape = (RELAY_SEGMENTS, 1, MIXER_HEADS)
    head_draw = jax.random.uniform(context_pieces[0], head_shape, jnp.float32)
    fast_rate = jax.random.uniform(context_pieces[1], head_shape, jnp.float32, 1.0 / 50.0, 1.0 / 30.0)
    middle_rate = jax.random.uniform(context_pieces[6], head_shape, jnp.float32, 1.35, 1.65) / TOK_DEV
    slow_rate = jax.random.uniform(context_pieces[2], head_shape, jnp.float32, 0.2, 1.0) / SEQUENCE_LENGTH
    head_rates = jnp.where(head_draw < fast_share, fast_rate, jnp.where(head_draw < fast_share + middle_share, middle_rate, slow_rate))
    jitter_level = jax.random.uniform(context_pieces[3], (RELAY_SEGMENTS, SEQUENCE_LENGTH, MIXER_HEADS), jnp.float32, 0.5, 1.5)
    spike_tokens = jax.random.randint(context_pieces[4], (RELAY_SEGMENTS, 1, 2), 0, SEQUENCE_LENGTH)
    token_positions = jnp.arange(SEQUENCE_LENGTH)[None, :, None]
    spike_hits = jnp.any(token_positions == spike_tokens, axis=2, keepdims=True)
    spike_depth = jax.random.uniform(context_pieces[5], head_shape, jnp.float32, 0.22, 0.51)
    decay_logs = -(head_rates * jitter_level) - jnp.where(spike_hits, spike_depth, 0.0)
    return (head_rates, decay_logs)


def draw_log_decay(key, part):
    return decay_plan(key)[1]


def draw_mix_input(key, part):
    head_rates, _ = decay_plan(key)
    noise_key = jax.random.fold_in(key, 31)
    noise_shape = (RELAY_SEGMENTS, SEQUENCE_LENGTH, MIXER_HEADS, SSD_DIM)
    noise = jnp.clip(jax.random.normal(noise_key, noise_shape, jnp.float32), -6.0, 6.0)
    floor_rate = jnp.maximum(head_rates, 1.0 / SEQUENCE_LENGTH)
    head_scale = jnp.sqrt(1.0 / (1.0 + 4.0 / (TOK_DEV * floor_rate)))
    scaled = noise * head_scale[..., None]
    return scaled.reshape(RELAY_SEGMENTS, SEQUENCE_LENGTH, MIXER_HEADS * SSD_DIM).astype(jnp.bfloat16)


def shard_levels(stream_key, shape, pieces, least, top_value):
    def one(dim, blocks):
        steps = jax.random.uniform(jax.random.fold_in(jax.random.fold_in(stream_key, 6), dim), (blocks,), jnp.float32, least / len(pieces), top_value / len(pieces))
        return jnp.repeat(jnp.exp(steps), shape[dim] // blocks).reshape((-1,) + (1,) * (len(shape) - dim - 1))

    gain = one(*pieces[0])
    for cut in pieces[1:]:
        gain = gain * one(*cut)
    return gain


def gaussian(stream_key, shape, deviation, bound, pieces=(), kind=jnp.bfloat16):
    result = jax.random.normal(stream_key, shape, jnp.float32) * deviation
    if len(pieces) > 0:
        result = shard_levels(stream_key, shape, pieces, -0.22, 0.18) * result
    return jnp.clip(result, min=-bound, max=bound).astype(kind)


def setup_inputs(seed: int = 0) -> dict:
    streams_of = jax.random.split(jax.random.key(seed), 11)
    mix_input = draw_mix_input(jax.random.fold_in(streams_of[10], 71), 0)
    state_write = gaussian(streams_of[1], (RELAY_SEGMENTS, SEQUENCE_LENGTH, NSTATE), ((NSTATE * TOK_DEV / 8) ** -0.25), 2.5, ((0, 4), (1, 4)))
    state_read = gaussian(streams_of[2], (RELAY_SEGMENTS, SEQUENCE_LENGTH, NSTATE), ((NSTATE * TOK_DEV / 8) ** -0.25), 2.5, ((0, 4), (1, 4)))
    log_decay = draw_log_decay(jax.random.fold_in(streams_of[10], 71), 0)
    skip_gain = jnp.clip(0.5 + 1.0 * jax.random.uniform(streams_of[4], (MIXER_HEADS,), jnp.float32) ** shard_levels(streams_of[4], (MIXER_HEADS,), ((0, 2),), -0.2, 0.2), 0.5, 1.5)
    query_rows = draw_query_rows(jax.random.fold_in(streams_of[10], 71), 0)
    key_rows = draw_key_rows(jax.random.fold_in(streams_of[10], 71), 0)
    value_rows = gaussian(streams_of[7], (RELAY_SEGMENTS, SEQUENCE_LENGTH, KV_HEADS * HEAD_DIM), 1.0, 6.0, ((0, 4), (1, 4), (2, 2)))
    incoming = gaussian(streams_of[8], (SEQUENCE_LENGTH, D), 1.0, 6.0, ((0, 4), (1, 2)))
    norm_gain = jnp.clip(1.0 + 0.1 * jax.random.normal(streams_of[9], (D,), jnp.float32), 0.5, 1.5)
    return dict(mix_input=mix_input, state_write=state_write, state_read=state_read, log_decay=log_decay, skip_gain=skip_gain, query_rows=query_rows, key_rows=key_rows, value_rows=value_rows, incoming=incoming, norm_gain=norm_gain)


def mix_segment(inputs, write_rows, read_rows, decays, skip_gain):
    heads_all = skip_gain.shape[0]
    values_in = inputs.astype(jnp.float32).reshape(inputs.shape[0], heads_all, -1)

    def advance(state_now, slices):
        token_in, write_one, read_one, decay_one = slices
        state_now = jnp.exp(decay_one)[:, None, None] * state_now + token_in[:, :, None] * write_one[None, None, :]
        output = jnp.einsum('hpn,n->hp', state_now, read_one, precision=lax.Precision.HIGHEST) + skip_gain[:, None] * token_in
        return (state_now, output)
    start_state = jnp.zeros((heads_all, values_in.shape[2], write_rows.shape[1]), jnp.float32)
    _, outputs = lax.scan(advance, start_state, (values_in, write_rows.astype(jnp.float32), read_rows.astype(jnp.float32), decays))
    return outputs.reshape(inputs.shape).astype(jnp.bfloat16)

def attend_segment(query_rows, key_rows, value_rows):
    seq_len = query_rows.shape[0]
    kv_count = key_rows.shape[1] // HEAD_DIM
    group_size = query_rows.shape[1] // (kv_count * HEAD_DIM)
    queries = query_rows.astype(jnp.float32).reshape(seq_len, kv_count, group_size, HEAD_DIM).transpose(1, 2, 0, 3)
    key_heads = key_rows.astype(jnp.float32).reshape(seq_len, kv_count, HEAD_DIM).transpose(1, 0, 2)
    value_heads = value_rows.astype(jnp.float32).reshape(seq_len, kv_count, HEAD_DIM).transpose(1, 0, 2)
    token_positions = jnp.arange(seq_len)
    allowed = token_positions[None, :] <= token_positions[:, None]

    def one_group(group_parts):
        query_group, key_group, value_group = group_parts
        scores = jnp.einsum('hto,so->hts', query_group, key_group) * HEAD_DIM ** (-0.5)
        masked = jnp.where(allowed, scores, -1e+30)
        row_max = lax.optimization_barrier(jnp.max(masked, axis=-1, keepdims=True))
        terms = jnp.where(allowed, jnp.exp(masked - row_max), 0.0)
        rounded = lax.optimization_barrier(terms.astype(jnp.bfloat16)).astype(jnp.float32)
        return jnp.einsum('hts,so->hto', rounded, value_group) / lax.optimization_barrier(jnp.sum(terms, axis=-1, keepdims=True))
    heads_out = lax.map(one_group, (queries, key_heads, value_heads))
    return heads_out.transpose(2, 0, 1, 3).reshape(seq_len, -1)

def reference(mix_input, state_write, state_read, log_decay, skip_gain, query_rows, key_rows, value_rows, incoming, norm_gain):
    mamba_out = lax.map(lambda segment_parts: mix_segment(segment_parts[0], segment_parts[1], segment_parts[2], segment_parts[3], skip_gain), (mix_input, state_write, state_read, log_decay))
    stream = jnp.concatenate([incoming[None], mamba_out[:-1]], axis=0)
    attention = lax.map(lambda segment_parts: attend_segment(segment_parts[0], segment_parts[1], segment_parts[2]), (query_rows, key_rows, value_rows))
    summed = stream.astype(jnp.float32) + attention
    squares = lax.optimization_barrier(jnp.sum(summed * summed, axis=-1, keepdims=True))
    block_out = (summed * lax.rsqrt(squares / D + 1e-05) * norm_gain).astype(jnp.bfloat16)
    return (mamba_out, block_out)
```

```python
import math

import jax
import jax.numpy as jnp
from jax import lax
from jax.experimental import pallas as pl
from jax.experimental.pallas import tpu as pltpu
from jax.sharding import PartitionSpec as P

D = 8192
HEAD_DIM = 128
LOG2E = 1.4426950408889634
F32 = jnp.float32
BF16 = jnp.bfloat16


def split_two(wide):
    upper = wide.astype(BF16)
    return upper, (wide - upper.astype(F32)).astype(BF16)


def dot32(a, b):
    return jnp.dot(a, b, preferred_element_type=F32)


def make_kernel(pipes, ranks, exps, tokens, heads, width, kv_width, nstate, chunk):
    size = width // heads
    chunks = width // chunk
    chunk_heads = chunk // size
    levels = ranks.bit_length() - 1
    kv_heads = kv_width // HEAD_DIM
    q_heads = width // HEAD_DIM
    group = q_heads // kv_heads
    together = math.gcd(4, group)
    keys = ranks * tokens

    def kernel(
        x_ref, write_ref, read_ref, decay_ref, skip_ref, q_ref, k_ref, v_ref, in_ref, gain_ref,
        mix_ref, out_ref,
        kbuf, vbuf, bias, stream, att, local, enter, outbox, inbox, spread_mat, cum_parts, cum_rows,
        pair_mat, dtot, dvec, tot_mine, tot_all, sq_mine, sq_all,
        st_send, st_recv, kv_send, kv_recv, tt_send, tt_recv, z_send, z_recv, e_send, e_recv,
    ):
        c = lax.axis_index("ctx")
        p = lax.axis_index("pipe")
        e = lax.axis_index("exp")

        def remote(src, dst, ssem, rsem, where):
            return pltpu.make_async_remote_copy(
                src_ref=src, dst_ref=dst, send_sem=ssem, recv_sem=rsem,
                device_id=where, device_id_type=pl.DeviceIdType.MESH,
            )

        barrier = pltpu.get_barrier_semaphore()
        for d in range(1, ranks):
            pl.semaphore_signal(barrier, inc=1, device_id={"ctx": lax.rem(c + d, ranks)},
                                device_id_type=pl.DeviceIdType.MESH)
        for d in range(1, exps):
            pl.semaphore_signal(barrier, inc=1, device_id={"exp": lax.rem(e + d, exps)},
                                device_id_type=pl.DeviceIdType.MESH)
        for d in (1, pipes - 1):
            pl.semaphore_signal(barrier, inc=1, device_id={"pipe": lax.rem(p + d, pipes)},
                                device_id_type=pl.DeviceIdType.MESH)

        rows = lax.broadcasted_iota(jnp.int32, (tokens, tokens), 0)
        cols = lax.broadcasted_iota(jnp.int32, (tokens, tokens), 1)
        tri = jnp.where(rows >= cols, 1.0, 0.0)
        cum = jnp.dot(tri, decay_ref[0] * LOG2E, precision=lax.Precision.HIGHEST,
                      preferred_element_type=F32)
        total = cum[tokens - 1:tokens, :]
        wide_cum = jnp.concatenate([cum, jnp.zeros((tokens, 128 - heads), F32)], axis=1)
        tot_mine[...] = jnp.broadcast_to(wide_cum[tokens - 1:tokens, :], tot_mine.shape)
        cum_rows[...] = jnp.transpose(wide_cum)
        for i in range(chunks):
            cum_parts[i] = wide_cum if i == 0 else pltpu.roll(wide_cum, 128 - i * chunk_heads, 1)
        spread_mat[...] = jnp.where(
            lax.broadcasted_iota(jnp.int32, (heads, width), 1) // size
            == lax.broadcasted_iota(jnp.int32, (heads, width), 0), 1.0, 0.0).astype(BF16)
        pairing = lax.dot_general(read_ref[0], write_ref[0], (((1,), (1,)), ((), ())),
                                  preferred_element_type=F32)
        pair_mat[...] = pairing * tri
        tail = split_two(jnp.exp2(total - cum))
        since = split_two(jnp.exp2(cum))
        skips = split_two(jnp.broadcast_to(skip_ref[...], (8, heads)))
        write_t = jnp.transpose(write_ref[0].astype(F32)).astype(BF16)

        pl.semaphore_wait(barrier, ranks - 1 + exps - 1 + 2)

        def tot_copy(d):
            return remote(tot_mine, tot_all.at[c], tt_send.at[d], tt_recv.at[c], {"ctx": c + d})

        for d in range(1, ranks):
            @pl.when(c + d < ranks)
            def _():
                tot_copy(d).start()

        def state_copy(level, d, i):
            at = pl.ds(pl.multiple_of(i * chunk, chunk), chunk)
            return remote(outbox.at[:, at], inbox.at[level, :, at], st_send.at[d, i],
                          st_recv.at[level, i], {"ctx": c + 1 + d})

        def sends_at(level):
            return lax.rem(c, 2 ** (level + 1)) == 2 ** level - 1

        def make_local(i, _):
            at = pl.ds(pl.multiple_of(i * chunk, chunk), chunk)
            mat = spread_mat[:, at]
            scaled = (dot32(tail[0], mat) + dot32(tail[1], mat)) * x_ref[0, :, at].astype(F32)
            state = dot32(write_t, scaled.astype(BF16))
            local[:, at] = state

            @pl.when(lax.rem(c, 2) == 0)
            def _():
                outbox[:, at] = state.astype(BF16)
                state_copy(0, 0, i).start()
            return 0

        lax.fori_loop(0, chunks, make_local, 0)

        def kv_copies(d):
            where = {"ctx": c + d}
            return (
                remote(k_ref.at[0], kbuf.at[c], kv_send.at[d, 0], kv_recv.at[c, 0], where),
                remote(v_ref.at[0], vbuf.at[c], kv_send.at[d, 1], kv_recv.at[c, 1], where),
            )

        for d in range(1, ranks):
            @pl.when(c + d < ranks)
            def _():
                for copy in kv_copies(d):
                    copy.start()

        for d in range(1, ranks):
            @pl.when(c >= d)
            def _():
                remote(tot_mine, tot_all.at[c - d], tt_send.at[d], tt_recv.at[c - d],
                       {"ctx": c}).wait_recv()
        def expand_row(logs):
            parts = split_two(jnp.exp2(logs)[:, :heads])
            return dot32(parts[0], spread_mat[...]) + dot32(parts[1], spread_mat[...])

        dtot[0] = expand_row(tot_mine[...])
        dtot[1] = dot32(skips[0], spread_mat[...]) + dot32(skips[1], spread_mat[...])
        for level in range(1, levels):
            base = (c // 2 ** level) * 2 ** level
            logs = jnp.zeros((8, 128), F32)
            for j in range(ranks):
                logs = logs + jnp.where((j >= base) & (j < c), tot_all[j], 0.0)
            dvec[level] = expand_row(logs)

        def receive(i):
            at = pl.ds(pl.multiple_of(i * chunk, chunk), chunk)
            enter[:, at] = jnp.zeros((nstate, chunk), F32)
            for level in range(levels):
                @pl.when(lax.rem(c // 2 ** level, 2) == 1)
                def _():
                    state_copy(level, 0, i).wait_recv()
                    got = inbox[level, :, at].astype(F32)
                    if level > 0:
                        got = dvec[level, 0:1, at] * got
                    enter[:, at] = enter[:, at] + got

        forwards = (lax.rem(c, 2) == 1) & (c < ranks - 1)

        @pl.when(forwards)
        def _():
            def forward(i, _):
                at = pl.ds(pl.multiple_of(i * chunk, chunk), chunk)
                receive(i)
                outbox[:, at] = (dtot[0, 0:1, at] * enter[:, at] + local[:, at]).astype(BF16)
                for level in range(1, levels):
                    @pl.when(sends_at(level))
                    def _():
                        for d in range(2 ** level):
                            state_copy(level, d, i).start()
                return 0
            lax.fori_loop(0, chunks, forward, 0)

        def onward(i):
            at = pl.ds(pl.multiple_of(i * chunk, chunk), chunk)
            return remote(mix_ref.at[0, :, at], stream.at[:, at], z_send.at[i], z_recv.at[i],
                          {"pipe": p + 1})

        lane = lax.broadcasted_iota(jnp.int32, (tokens, 2 * size), 1)

        def finish_mix(i, _):
            at = pl.ds(pl.multiple_of(i * chunk, chunk), chunk)

            @pl.when(jnp.logical_not(forwards))
            def _():
                receive(i)

            mat = spread_mat[:, at]
            grown = dot32(since[0], mat) + dot32(since[1], mat)
            outer = grown * dot32(read_ref[0], enter[:, at].astype(BF16))
            outer = outer + dtot[1, 0:1, at] * x_ref[0, :, at].astype(F32)
            columns = cum_parts[i]
            lines = cum_rows[pl.ds(pl.multiple_of(i * chunk_heads, chunk_heads), chunk_heads), :]
            inner = []
            for k in range(0, chunk_heads, 2):
                both = []
                for h in (k, k + 1):
                    spread = jnp.minimum(columns[:, h:h + 1] - lines[h:h + 1, :], 0.0)
                    both.append((jnp.exp2(spread) * pair_mat[...]).astype(BF16))
                start = pl.multiple_of(i * chunk + k * size, 2 * size)
                xs = x_ref[0, :, pl.ds(start, 2 * size)]
                zero = jnp.zeros_like(xs)
                halves = jnp.concatenate(
                    [jnp.where(lane < size, xs, zero), jnp.where(lane < size, zero, xs)], axis=0)
                inner.append(dot32(jnp.concatenate(both, axis=1), halves))
            mix_ref[0, :, at] = (jnp.concatenate(inner, axis=1) + outer).astype(BF16)

            @pl.when(p < pipes - 1)
            def _():
                onward(i).start()
            return 0

        lax.fori_loop(0, chunks, finish_mix, 0)

        @pl.when(p == 0)
        def _():
            stream[...] = in_ref[...]

        kbuf[c] = k_ref[0]
        vbuf[c] = v_ref[0]
        for j in range(1, ranks):
            @pl.when(j > c)
            def _():
                kbuf[j] = jnp.zeros(kbuf.shape[1:], BF16)
                vbuf[j] = jnp.zeros(vbuf.shape[1:], BF16)
        bias[...] = jnp.where(
            lax.broadcasted_iota(jnp.int32, (tokens, keys), 1)
            <= c * tokens + lax.broadcasted_iota(jnp.int32, (tokens, keys), 0), 0.0, -1e30)
        for d in range(1, ranks):
            @pl.when(c >= d)
            def _():
                where = {"ctx": c}
                remote(k_ref.at[0], kbuf.at[c - d], kv_send.at[d, 0], kv_recv.at[c - d, 0], where).wait_recv()
                remote(v_ref.at[0], vbuf.at[c - d], kv_send.at[d, 1], kv_recv.at[c - d, 1], where).wait_recv()

        def attend(step, _):
            for r in range(together):
                h = step * together + r
                at = pl.ds(pl.multiple_of(h * HEAD_DIM, HEAD_DIM), HEAD_DIM)
                g = (step * together) // group
                kv_at = pl.ds(pl.multiple_of(g * HEAD_DIM, HEAD_DIM), HEAD_DIM)
                kk = kbuf[:, :, kv_at].reshape(keys, HEAD_DIM)
                vv = vbuf[:, :, kv_at].reshape(keys, HEAD_DIM)
                s = lax.dot_general(q_ref[0, :, at], kk, (((1,), (1,)), ((), ())),
                                    preferred_element_type=F32)
                s = s * (LOG2E * HEAD_DIM ** -0.5) + bias[...]
                terms = jnp.exp2(s - jnp.max(s, axis=1, keepdims=True))
                weighted = dot32(terms.astype(BF16), vv)
                att[:, at] = weighted * (1.0 / jnp.sum(terms, axis=1, keepdims=True))
            return 0

        lax.fori_loop(0, q_heads // together, attend, 0)

        sq_mine[...] = jnp.zeros_like(sq_mine)

        def add_up(i, _):
            at = pl.ds(pl.multiple_of(i * chunk, chunk), chunk)

            @pl.when(p > 0)
            def _():
                onward(i).wait_recv()
            summed = stream[:, at].astype(F32) + att[:, at]
            att[:, at] = summed
            square = summed * summed
            part = square[:, :128]
            for k in range(1, chunk // 128):
                part = part + square[:, k * 128:(k + 1) * 128]
            sq_mine[...] += part
            return 0

        lax.fori_loop(0, chunks, add_up, 0)
        swaps = [
            remote(sq_mine, sq_all.at[d - 1], e_send.at[d - 1], e_recv.at[d - 1],
                   {"exp": lax.rem(e + d, exps)})
            for d in range(1, exps)
        ]
        for copy in swaps:
            copy.start()
        for copy in swaps:
            copy.wait()
        squares = sq_mine[...]
        for d in range(exps - 1):
            squares = squares + sq_all[d]
        factor = lax.rsqrt(jnp.sum(squares, axis=1, keepdims=True) / D + 1e-05)

        def scale(i, _):
            at = pl.ds(pl.multiple_of(i * chunk, chunk), chunk)
            out_ref[0, :, at] = (att[:, at] * factor * gain_ref[0:1, at]).astype(BF16)
            return 0

        lax.fori_loop(0, chunks, scale, 0)

        for d in range(1, ranks):
            @pl.when(c + d < ranks)
            def _():
                tot_copy(d).wait_send()
                for copy in kv_copies(d):
                    copy.wait_send()
        for level in range(levels):
            @pl.when(sends_at(level))
            def _():
                def drain(i, _):
                    for d in range(2 ** level):
                        state_copy(level, d, i).wait_send()
                    return 0
                lax.fori_loop(0, chunks, drain, 0)

        @pl.when(p < pipes - 1)
        def _():
            def drain(i, _):
                onward(i).wait_send()
                return 0
            lax.fori_loop(0, chunks, drain, 0)

    scratch = [
        pltpu.VMEM((ranks, tokens, kv_width), BF16),
        pltpu.VMEM((ranks, tokens, kv_width), BF16),
        pltpu.VMEM((tokens, keys), F32),
        pltpu.VMEM((tokens, width), BF16),
        pltpu.VMEM((tokens, width), F32),
        pltpu.VMEM((nstate, width), F32),
        pltpu.VMEM((nstate, width), F32),
        pltpu.VMEM((nstate, width), BF16),
        pltpu.VMEM((levels, nstate, width), BF16),
        pltpu.VMEM((heads, width), BF16),
        pltpu.VMEM((chunks, tokens, 128), F32),
        pltpu.VMEM((128, tokens), F32),
        pltpu.VMEM((tokens, tokens), F32),
        pltpu.VMEM((2, 8, width), F32),
        pltpu.VMEM((levels, 8, width), F32),
        pltpu.VMEM((8, 128), F32),
        pltpu.VMEM((ranks, 8, 128), F32),
        pltpu.VMEM((tokens, 128), F32),
        pltpu.VMEM((max(exps - 1, 1), tokens, 128), F32),
        pltpu.SemaphoreType.DMA((ranks // 2, chunks)),
        pltpu.SemaphoreType.DMA((levels, chunks)),
        pltpu.SemaphoreType.DMA((ranks, 2)),
        pltpu.SemaphoreType.DMA((ranks, 2)),
        pltpu.SemaphoreType.DMA((ranks,)),
        pltpu.SemaphoreType.DMA((ranks,)),
        pltpu.SemaphoreType.DMA((chunks,)),
        pltpu.SemaphoreType.DMA((chunks,)),
        pltpu.SemaphoreType.DMA((exps,)),
        pltpu.SemaphoreType.DMA((exps,)),
    ]
    return kernel, scratch


def solution(mesh):
    pipes, ranks, exps = (mesh.shape[a] for a in ("pipe", "ctx", "exp"))

    def body(
        mix_input, state_write, state_read, log_decay, skip_gain, query_rows, key_rows,
        value_rows, incoming, norm_gain,
    ):
        tokens, width = mix_input.shape[1:]
        heads = skip_gain.shape[0]
        kernel, scratch = make_kernel(
            pipes, ranks, exps, tokens, heads, width, key_rows.shape[2], state_write.shape[2], 512)
        vmem = pl.BlockSpec(memory_space=pltpu.VMEM)
        shape = jax.ShapeDtypeStruct(mix_input.shape, BF16)
        return pl.pallas_call(
            kernel,
            out_shape=(shape, shape),
            in_specs=[vmem] * 10,
            out_specs=(vmem, vmem),
            scratch_shapes=scratch,
            compiler_params=pltpu.CompilerParams(
                collective_id=0, has_side_effects=True, vmem_limit_bytes=48 * 2 ** 20),
        )(mix_input, state_write, state_read, log_decay, skip_gain[None], query_rows, key_rows,
          value_rows, incoming, norm_gain[None])

    placed = (
        P("pipe", "ctx", "exp"), P("pipe", "ctx", None), P("pipe", "ctx", None),
        P("pipe", "ctx", "exp"), P("exp"), P("pipe", "ctx", "exp"), P("pipe", "ctx", "exp"),
        P("pipe", "ctx", "exp"), P("ctx", "exp"), P("exp"),
    )
    return jax.shard_map(
        body, mesh=mesh, in_specs=placed,
        out_specs=(P("pipe", "ctx", "exp"), P("pipe", "ctx", "exp")), check_vma=False,
    )
```

```python
import jax
import jax.numpy as jnp
from jax import lax
from jax.experimental import pallas as pl
from jax.experimental.pallas import tpu as pltpu
from jax.sharding import PartitionSpec as P

D = 8192
HEAD_DIM = 128
LOG2E = 1.4426950408889634
F32 = jnp.float32
BF16 = jnp.bfloat16


def split_two(wide):
    upper = wide.astype(BF16)
    return upper, (wide - upper.astype(F32)).astype(BF16)


def dot32(a, b):
    return jnp.dot(a, b, preferred_element_type=F32)


def make_kernel(pipes, ranks, exps, tokens, heads, width, kv_width, nstate, chunk):
    size = width // heads
    chunks = width // chunk
    chunk_heads = chunk // size
    levels = ranks.bit_length() - 1
    kv_heads = kv_width // HEAD_DIM
    q_heads = width // HEAD_DIM
    keys = ranks * tokens

    def kernel(
        x_hbm, write_hbm, read_hbm, decay_hbm, skip_hbm, q_hbm, k_hbm, v_hbm, in_hbm, gain_hbm,
        mix_ref, out_ref,
        x_ref, write_ref, read_ref, decay_ref, skip_ref, q_ref, gain_ref, in_sem, x_sem, kv_sem,
        kbuf, vbuf, bias, stream, att, local, enter, outbox, inbox, spread_mat, cum_parts, cum_rows,
        pair_mat, dtot, dvec, tot_mine, tot_all, sq_mine, sq_all,
        st_send, st_recv, kv_send, kv_recv, tt_send, tt_recv, z_send, z_recv, e_send, e_recv,
    ):
        c = lax.axis_index("ctx")
        p = lax.axis_index("pipe")
        e = lax.axis_index("exp")

        def remote(src, dst, ssem, rsem, where):
            return pltpu.make_async_remote_copy(
                src_ref=src, dst_ref=dst, send_sem=ssem, recv_sem=rsem,
                device_id=where, device_id_type=pl.DeviceIdType.MESH,
            )

        small = [
            pltpu.make_async_copy(src, dst, in_sem.at[i])
            for i, (src, dst) in enumerate((
                (decay_hbm.at[0], decay_ref), (write_hbm.at[0], write_ref),
                (read_hbm.at[0], read_ref), (skip_hbm, skip_ref), (gain_hbm, gain_ref)))
        ]
        for copy in small:
            copy.start()

        def own_kv(g):
            at = pl.ds(pl.multiple_of(g * HEAD_DIM, HEAD_DIM), HEAD_DIM)
            return (pltpu.make_async_copy(k_hbm.at[0, :, at], kbuf.at[c, g], kv_sem.at[g, 0]),
                    pltpu.make_async_copy(v_hbm.at[0, :, at], vbuf.at[c, g], kv_sem.at[g, 1]))

        def own_x(i):
            at = pl.ds(pl.multiple_of(i * chunk, chunk), chunk)
            return pltpu.make_async_copy(x_hbm.at[0, :, at], x_ref.at[:, at], x_sem.at[i])

        for g in range(kv_heads):
            for copy in own_kv(g):
                copy.start()
        for i in range(chunks):
            own_x(i).start()
        q_copy = pltpu.make_async_copy(q_hbm.at[0], q_ref, in_sem.at[5])
        q_copy.start()
        in_copy = pltpu.make_async_copy(in_hbm, stream, in_sem.at[6])

        @pl.when(p == 0)
        def _():
            in_copy.start()

        barrier = pltpu.get_barrier_semaphore()
        for d in range(1, ranks):
            pl.semaphore_signal(barrier, inc=1, device_id={"ctx": lax.rem(c + d, ranks)},
                                device_id_type=pl.DeviceIdType.MESH)
        for d in range(1, exps):
            pl.semaphore_signal(barrier, inc=1, device_id={"exp": lax.rem(e + d, exps)},
                                device_id_type=pl.DeviceIdType.MESH)
        for d in (1, pipes - 1):
            pl.semaphore_signal(barrier, inc=1, device_id={"pipe": lax.rem(p + d, pipes)},
                                device_id_type=pl.DeviceIdType.MESH)

        rows = lax.broadcasted_iota(jnp.int32, (tokens, tokens), 0)
        cols = lax.broadcasted_iota(jnp.int32, (tokens, tokens), 1)
        tri = jnp.where(rows >= cols, 1.0, 0.0)
        spread_mat[...] = jnp.where(
            lax.broadcasted_iota(jnp.int32, (heads, width), 1) // size
            == lax.broadcasted_iota(jnp.int32, (heads, width), 0), 1.0, 0.0).astype(BF16)
        for copy in small:
            copy.wait()
        by_token = jnp.transpose(jnp.concatenate(
            [decay_ref[...] * LOG2E, jnp.zeros((128 - heads, tokens), F32)], axis=0))
        wide_cum = jnp.dot(tri, by_token, precision=lax.Precision.HIGHEST,
                           preferred_element_type=F32)
        cum = wide_cum[:, :heads]
        total = cum[tokens - 1:tokens, :]
        tot_mine[...] = jnp.broadcast_to(wide_cum[tokens - 1:tokens, :], tot_mine.shape)
        cum_rows[...] = jnp.transpose(wide_cum)
        for i in range(chunks):
            cum_parts[i] = wide_cum if i == 0 else pltpu.roll(wide_cum, 128 - i * chunk_heads, 1)
        read_rows = jnp.transpose(read_ref[...].astype(F32)).astype(BF16)
        pair_mat[...] = dot32(read_rows, write_ref[...]) * tri
        tail = split_two(jnp.exp2(total - cum))
        since = split_two(jnp.exp2(cum))
        skips = split_two(jnp.broadcast_to(skip_ref[...], (8, heads)))

        pl.semaphore_wait(barrier, ranks - 1 + exps - 1 + 2)

        def tot_copy(d):
            return remote(tot_mine, tot_all.at[c], tt_send.at[d], tt_recv.at[c], {"ctx": c + d})

        for d in range(1, ranks):
            @pl.when(c + d < ranks)
            def _():
                tot_copy(d).start()

        def state_copy(level, d, i):
            at = pl.ds(pl.multiple_of(i * chunk, chunk), chunk)
            return remote(outbox.at[:, at], inbox.at[level, :, at], st_send.at[d, i],
                          st_recv.at[level, i], {"ctx": c + 1 + d})

        def sends_at(level):
            return lax.rem(c, 2 ** (level + 1)) == 2 ** level - 1

        def kv_copies(d, g):
            where = {"ctx": c + d}
            return (
                remote(kbuf.at[c, g], kbuf.at[c, g], kv_send.at[d, g, 0], kv_recv.at[c, g, 0], where),
                remote(vbuf.at[c, g], vbuf.at[c, g], kv_send.at[d, g, 1], kv_recv.at[c, g, 1], where),
            )

        def wait_kv(d, g):
            where = {"ctx": c}
            j = c - d
            remote(kbuf.at[j, g], kbuf.at[j, g], kv_send.at[d, g, 0], kv_recv.at[j, g, 0], where).wait_recv()
            remote(vbuf.at[j, g], vbuf.at[j, g], kv_send.at[d, g, 1], kv_recv.at[j, g, 1], where).wait_recv()

        def make_local(i, _):
            at = pl.ds(pl.multiple_of(i * chunk, chunk), chunk)
            own_x(i).wait()
            mat = spread_mat[:, at]
            scaled = (dot32(tail[0], mat) + dot32(tail[1], mat)) * x_ref[:, at].astype(F32)
            state = dot32(write_ref[...], scaled.astype(BF16))
            local[:, at] = state

            @pl.when(lax.rem(c, 2) == 0)
            def _():
                outbox[:, at] = state.astype(BF16)
                state_copy(0, 0, i).start()

            @pl.when(lax.rem(i, chunks // kv_heads) == 0)
            def _():
                g = i // (chunks // kv_heads)
                for copy in own_kv(g):
                    copy.wait()
                for d in range(1, ranks):
                    @pl.when(c + d < ranks)
                    def _():
                        for copy in kv_copies(d, g):
                            copy.start()
            return 0

        lax.fori_loop(0, chunks, make_local, 0)

        for d in range(1, ranks):
            @pl.when(c >= d)
            def _():
                remote(tot_mine, tot_all.at[c - d], tt_send.at[d], tt_recv.at[c - d],
                       {"ctx": c}).wait_recv()
        def expand_row(logs):
            parts = split_two(jnp.exp2(logs)[:, :heads])
            return dot32(parts[0], spread_mat[...]) + dot32(parts[1], spread_mat[...])

        dtot[0] = expand_row(tot_mine[...])
        dtot[1] = dot32(skips[0], spread_mat[...]) + dot32(skips[1], spread_mat[...])
        for level in range(1, levels):
            base = (c // 2 ** level) * 2 ** level
            logs = jnp.zeros((8, 128), F32)
            for j in range(ranks):
                logs = logs + jnp.where((j >= base) & (j < c), tot_all[j], 0.0)
            dvec[level] = expand_row(logs)

        def receive(i):
            at = pl.ds(pl.multiple_of(i * chunk, chunk), chunk)
            enter[:, at] = jnp.zeros((nstate, chunk), F32)
            for level in range(levels):
                @pl.when(lax.rem(c // 2 ** level, 2) == 1)
                def _():
                    state_copy(level, 0, i).wait_recv()
                    got = inbox[level, :, at].astype(F32)
                    if level > 0:
                        got = dvec[level, 0:1, at] * got
                    enter[:, at] = enter[:, at] + got

        forwards = (lax.rem(c, 2) == 1) & (c < ranks - 1)

        def onward(i):
            at = pl.ds(pl.multiple_of(i * chunk, chunk), chunk)
            return remote(mix_ref.at[0, :, at], stream.at[:, at], z_send.at[i], z_recv.at[i],
                          {"pipe": p + 1})

        lane = lax.broadcasted_iota(jnp.int32, (tokens, 2 * size), 1)

        def finish_mix(i, _):
            at = pl.ds(pl.multiple_of(i * chunk, chunk), chunk)

            receive(i)

            @pl.when(forwards)
            def _():
                outbox[:, at] = (dtot[0, 0:1, at] * enter[:, at] + local[:, at]).astype(BF16)
                for level in range(1, levels):
                    @pl.when(sends_at(level))
                    def _():
                        for d in range(2 ** level):
                            state_copy(level, d, i).start()

            mat = spread_mat[:, at]
            grown = dot32(since[0], mat) + dot32(since[1], mat)
            outer = grown * dot32(read_rows, enter[:, at].astype(BF16))
            outer = outer + dtot[1, 0:1, at] * x_ref[:, at].astype(F32)
            columns = cum_parts[i]
            lines = cum_rows[pl.ds(pl.multiple_of(i * chunk_heads, chunk_heads), chunk_heads), :]
            inner = []
            for k in range(0, chunk_heads, 2):
                both = []
                for h in (k, k + 1):
                    spread = jnp.minimum(columns[:, h:h + 1] - lines[h:h + 1, :], 0.0)
                    both.append((jnp.exp2(spread) * pair_mat[...]).astype(BF16))
                start = pl.multiple_of(i * chunk + k * size, 2 * size)
                xs = x_ref[:, pl.ds(start, 2 * size)]
                zero = jnp.zeros_like(xs)
                halves = jnp.concatenate(
                    [jnp.where(lane < size, xs, zero), jnp.where(lane < size, zero, xs)], axis=0)
                inner.append(dot32(jnp.concatenate(both, axis=1), halves))
            mix_ref[0, :, at] = (jnp.concatenate(inner, axis=1) + outer).astype(BF16)

            @pl.when(p < pipes - 1)
            def _():
                onward(i).start()
            return 0

        for j in range(1, ranks):
            @pl.when(j > c)
            def _():
                kbuf[j] = jnp.zeros(kbuf.shape[1:], BF16)
                vbuf[j] = jnp.zeros(vbuf.shape[1:], BF16)
        bias[...] = jnp.where(
            lax.broadcasted_iota(jnp.int32, (tokens, keys), 1)
            <= c * tokens + lax.broadcasted_iota(jnp.int32, (tokens, keys), 0), 0.0, -1e30)
        q_copy.wait()

        def attend(i):
            g = i // (chunks // kv_heads)

            @pl.when(lax.rem(i, chunks // kv_heads) == 0)
            def _():
                for d in range(1, ranks):
                    @pl.when(c >= d)
                    def _():
                        wait_kv(d, g)
            kk = kbuf[:, g].reshape(keys, HEAD_DIM)
            vv = vbuf[:, g].reshape(keys, HEAD_DIM)
            for r in range(chunk // HEAD_DIM):
                at = pl.ds(pl.multiple_of(i * chunk + r * HEAD_DIM, HEAD_DIM), HEAD_DIM)
                s = lax.dot_general(q_ref[:, at], kk, (((1,), (1,)), ((), ())),
                                    preferred_element_type=F32)
                s = s * (LOG2E * HEAD_DIM ** -0.5) + bias[...]
                terms = jnp.exp2(s - jnp.max(s, axis=1, keepdims=True))
                weighted = dot32(terms.astype(BF16), vv)
                att[:, at] = weighted * (1.0 / jnp.sum(terms, axis=1, keepdims=True))

        def main(i, _):
            finish_mix(i, 0)
            attend(i)
            return 0

        lax.fori_loop(0, chunks, main, 0)

        @pl.when(p == 0)
        def _():
            in_copy.wait()

        sq_mine[...] = jnp.zeros_like(sq_mine)

        def add_up(i, _):
            at = pl.ds(pl.multiple_of(i * chunk, chunk), chunk)

            @pl.when(p > 0)
            def _():
                onward(i).wait_recv()
            summed = stream[:, at].astype(F32) + att[:, at]
            att[:, at] = summed
            square = summed * summed
            part = square[:, :128]
            for k in range(1, chunk // 128):
                part = part + square[:, k * 128:(k + 1) * 128]
            sq_mine[...] += part
            return 0

        lax.fori_loop(0, chunks, add_up, 0)
        swaps = [
            remote(sq_mine, sq_all.at[d - 1], e_send.at[d - 1], e_recv.at[d - 1],
                   {"exp": lax.rem(e + d, exps)})
            for d in range(1, exps)
        ]
        for copy in swaps:
            copy.start()
        for copy in swaps:
            copy.wait()
        squares = sq_mine[...]
        for d in range(exps - 1):
            squares = squares + sq_all[d]
        factor = lax.rsqrt(jnp.sum(squares, axis=1, keepdims=True) / D + 1e-05)

        def scale(i, _):
            at = pl.ds(pl.multiple_of(i * chunk, chunk), chunk)
            out_ref[0, :, at] = (att[:, at] * factor * gain_ref[0:1, at]).astype(BF16)
            return 0

        lax.fori_loop(0, chunks, scale, 0)

        for d in range(1, ranks):
            @pl.when(c + d < ranks)
            def _():
                tot_copy(d).wait_send()
                for g in range(kv_heads):
                    for copy in kv_copies(d, g):
                        copy.wait_send()
        for level in range(levels):
            @pl.when(sends_at(level))
            def _():
                def drain(i, _):
                    for d in range(2 ** level):
                        state_copy(level, d, i).wait_send()
                    return 0
                lax.fori_loop(0, chunks, drain, 0)

        @pl.when(p < pipes - 1)
        def _():
            def drain(i, _):
                onward(i).wait_send()
                return 0
            lax.fori_loop(0, chunks, drain, 0)

    scratch = [
        pltpu.VMEM((tokens, width), BF16),
        pltpu.VMEM((nstate, tokens), BF16),
        pltpu.VMEM((nstate, tokens), BF16),
        pltpu.VMEM((heads, tokens), F32),
        pltpu.VMEM((1, heads), F32),
        pltpu.VMEM((tokens, width), BF16),
        pltpu.VMEM((1, width), F32),
        pltpu.SemaphoreType.DMA((7,)),
        pltpu.SemaphoreType.DMA((chunks,)),
        pltpu.SemaphoreType.DMA((kv_heads, 2)),
        pltpu.VMEM((ranks, kv_heads, tokens, HEAD_DIM), BF16),
        pltpu.VMEM((ranks, kv_heads, tokens, HEAD_DIM), BF16),
        pltpu.VMEM((tokens, keys), F32),
        pltpu.VMEM((tokens, width), BF16),
        pltpu.VMEM((tokens, width), F32),
        pltpu.VMEM((nstate, width), F32),
        pltpu.VMEM((nstate, width), F32),
        pltpu.VMEM((nstate, width), BF16),
        pltpu.VMEM((levels, nstate, width), BF16),
        pltpu.VMEM((heads, width), BF16),
        pltpu.VMEM((chunks, tokens, 128), F32),
        pltpu.VMEM((128, tokens), F32),
        pltpu.VMEM((tokens, tokens), F32),
        pltpu.VMEM((2, 8, width), F32),
        pltpu.VMEM((levels, 8, width), F32),
        pltpu.VMEM((8, 128), F32),
        pltpu.VMEM((ranks, 8, 128), F32),
        pltpu.VMEM((tokens, 128), F32),
        pltpu.VMEM((max(exps - 1, 1), tokens, 128), F32),
        pltpu.SemaphoreType.DMA((ranks // 2, chunks)),
        pltpu.SemaphoreType.DMA((levels, chunks)),
        pltpu.SemaphoreType.DMA((ranks, kv_heads, 2)),
        pltpu.SemaphoreType.DMA((ranks, kv_heads, 2)),
        pltpu.SemaphoreType.DMA((ranks,)),
        pltpu.SemaphoreType.DMA((ranks,)),
        pltpu.SemaphoreType.DMA((chunks,)),
        pltpu.SemaphoreType.DMA((chunks,)),
        pltpu.SemaphoreType.DMA((exps,)),
        pltpu.SemaphoreType.DMA((exps,)),
    ]
    return kernel, scratch


def solution(mesh):
    pipes, ranks, exps = (mesh.shape[a] for a in ("pipe", "ctx", "exp"))

    def body(
        mix_input, state_write, state_read, log_decay, skip_gain, query_rows, key_rows,
        value_rows, incoming, norm_gain,
    ):
        tokens, width = mix_input.shape[1:]
        heads = skip_gain.shape[0]
        kernel, scratch = make_kernel(
            pipes, ranks, exps, tokens, heads, width, key_rows.shape[2], state_write.shape[2], 512)
        vmem = pl.BlockSpec(memory_space=pltpu.VMEM)
        shape = jax.ShapeDtypeStruct(mix_input.shape, BF16)
        return pl.pallas_call(
            kernel,
            out_shape=(shape, shape),
            in_specs=[pl.BlockSpec(memory_space=pltpu.HBM)] * 10,
            out_specs=(vmem, vmem),
            scratch_shapes=scratch,
            compiler_params=pltpu.CompilerParams(
                collective_id=0, has_side_effects=True, vmem_limit_bytes=60 * 2 ** 20),
        )(mix_input, jnp.swapaxes(state_write, 1, 2), jnp.swapaxes(state_read, 1, 2),
          jnp.swapaxes(log_decay, 1, 2), skip_gain[None], query_rows, key_rows,
          value_rows, incoming, norm_gain[None])

    placed = (
        P("pipe", "ctx", "exp"), P("pipe", "ctx", None), P("pipe", "ctx", None),
        P("pipe", "ctx", "exp"), P("exp"), P("pipe", "ctx", "exp"), P("pipe", "ctx", "exp"),
        P("pipe", "ctx", "exp"), P("ctx", "exp"), P("exp"),
    )
    return jax.shard_map(
        body, mesh=mesh, in_specs=placed,
        out_specs=(P("pipe", "ctx", "exp"), P("pipe", "ctx", "exp")), check_vma=False,
    )
```

```python
import jax
import jax.numpy as jnp
from jax import lax
from jax.experimental import pallas as pl
from jax.experimental.pallas import tpu as pltpu
from jax.sharding import PartitionSpec as P

D = 8192
HEAD_DIM = 128
LOG2E = 1.4426950408889634
F32 = jnp.float32
BF16 = jnp.bfloat16


def split_two(wide):
    upper = wide.astype(BF16)
    return upper, (wide - upper.astype(F32)).astype(BF16)


def dot32(a, b):
    return jnp.dot(a, b, preferred_element_type=F32)


def make_kernel(pipes, ranks, exps, tokens, heads, width, kv_width, nstate, chunk):
    size = width // heads
    chunks = width // chunk
    chunk_heads = chunk // size
    levels = ranks.bit_length() - 1
    kv_heads = kv_width // HEAD_DIM
    q_heads = width // HEAD_DIM
    keys = ranks * tokens

    def kernel(
        x_hbm, write_hbm, read_hbm, decay_hbm, skip_hbm, q_hbm, k_hbm, v_hbm, in_hbm, gain_hbm,
        mix_ref, out_ref,
        x_ref, write_ref, read_ref, decay_ref, skip_ref, q_ref, gain_ref, in_sem, x_sem, kv_sem,
        kbuf, vbuf, bias, stream, att, local, enter, outbox, inbox, spread_mat, cum_parts, cum_rows,
        pair_mat, dtot, dvec, tot_mine, tot_all, sq_mine, sq_all,
        st_send, st_recv, kv_send, kv_recv, tt_send, tt_recv, z_send, z_recv, e_send, e_recv,
    ):
        c = lax.axis_index("ctx")
        p = lax.axis_index("pipe")
        e = lax.axis_index("exp")

        def remote(src, dst, ssem, rsem, where):
            return pltpu.make_async_remote_copy(
                src_ref=src, dst_ref=dst, send_sem=ssem, recv_sem=rsem,
                device_id=where, device_id_type=pl.DeviceIdType.MESH,
            )

        small = [
            pltpu.make_async_copy(src, dst, in_sem.at[i])
            for i, (src, dst) in enumerate((
                (decay_hbm.at[0], decay_ref), (write_hbm.at[0], write_ref),
                (read_hbm.at[0], read_ref), (skip_hbm, skip_ref), (gain_hbm, gain_ref)))
        ]
        for copy in small:
            copy.start()

        def own_kv(g):
            at = pl.ds(pl.multiple_of(g * HEAD_DIM, HEAD_DIM), HEAD_DIM)
            return (pltpu.make_async_copy(k_hbm.at[0, :, at], kbuf.at[c, g], kv_sem.at[g, 0]),
                    pltpu.make_async_copy(v_hbm.at[0, :, at], vbuf.at[c, g], kv_sem.at[g, 1]))

        def own_x(i):
            at = pl.ds(pl.multiple_of(i * chunk, chunk), chunk)
            return pltpu.make_async_copy(x_hbm.at[0, :, at], x_ref.at[:, at], x_sem.at[i])

        for g in range(kv_heads):
            for copy in own_kv(g):
                copy.start()
        for i in range(chunks):
            own_x(i).start()
        q_copy = pltpu.make_async_copy(q_hbm.at[0], q_ref, in_sem.at[5])
        q_copy.start()
        in_copy = pltpu.make_async_copy(in_hbm, stream, in_sem.at[6])

        @pl.when(p == 0)
        def _():
            in_copy.start()

        barrier = pltpu.get_barrier_semaphore()
        for d in range(1, ranks):
            pl.semaphore_signal(barrier, inc=1, device_id={"ctx": lax.rem(c + d, ranks)},
                                device_id_type=pl.DeviceIdType.MESH)
        for d in range(1, exps):
            pl.semaphore_signal(barrier, inc=1, device_id={"exp": lax.rem(e + d, exps)},
                                device_id_type=pl.DeviceIdType.MESH)
        for d in (1, pipes - 1):
            pl.semaphore_signal(barrier, inc=1, device_id={"pipe": lax.rem(p + d, pipes)},
                                device_id_type=pl.DeviceIdType.MESH)

        rows = lax.broadcasted_iota(jnp.int32, (tokens, tokens), 0)
        cols = lax.broadcasted_iota(jnp.int32, (tokens, tokens), 1)
        tri = jnp.where(rows >= cols, 1.0, 0.0)
        spread_mat[...] = jnp.where(
            lax.broadcasted_iota(jnp.int32, (heads, width), 1) // size
            == lax.broadcasted_iota(jnp.int32, (heads, width), 0), 1.0, 0.0).astype(BF16)
        for copy in small:
            copy.wait()
        by_token = jnp.transpose(jnp.concatenate(
            [decay_ref[...] * LOG2E, jnp.zeros((128 - heads, tokens), F32)], axis=0))
        wide_cum = jnp.dot(tri, by_token, precision=lax.Precision.HIGHEST,
                           preferred_element_type=F32)
        cum = wide_cum[:, :heads]
        total = cum[tokens - 1:tokens, :]
        tot_mine[...] = jnp.broadcast_to(wide_cum[tokens - 1:tokens, :], tot_mine.shape)
        cum_rows[...] = jnp.transpose(wide_cum)
        for i in range(chunks):
            cum_parts[i] = wide_cum if i == 0 else pltpu.roll(wide_cum, 128 - i * chunk_heads, 1)
        read_rows = jnp.transpose(read_ref[...].astype(F32)).astype(BF16)
        pair_mat[...] = dot32(read_rows, write_ref[...]) * tri
        tail = split_two(jnp.exp2(total - cum))
        since = split_two(jnp.exp2(cum))
        skips = split_two(jnp.broadcast_to(skip_ref[...], (8, heads)))

        pl.semaphore_wait(barrier, ranks - 1 + exps - 1 + 2)

        def tot_copy(d):
            return remote(tot_mine, tot_all.at[c], tt_send.at[d], tt_recv.at[c], {"ctx": c + d})

        for d in range(1, ranks):
            @pl.when(c + d < ranks)
            def _():
                tot_copy(d).start()

        def state_copy(level, d, i):
            at = pl.ds(pl.multiple_of(i * chunk, chunk), chunk)
            return remote(outbox.at[:, at], inbox.at[level, :, at], st_send.at[d, i],
                          st_recv.at[level, i], {"ctx": c + 1 + d})

        def sends_at(level):
            return lax.rem(c, 2 ** (level + 1)) == 2 ** level - 1

        def kv_copies(d, g):
            where = {"ctx": c + d}
            return (
                remote(kbuf.at[c, g], kbuf.at[c, g], kv_send.at[d, g, 0], kv_recv.at[c, g, 0], where),
                remote(vbuf.at[c, g], vbuf.at[c, g], kv_send.at[d, g, 1], kv_recv.at[c, g, 1], where),
            )

        def wait_kv(d, g):
            where = {"ctx": c}
            j = c - d
            remote(kbuf.at[j, g], kbuf.at[j, g], kv_send.at[d, g, 0], kv_recv.at[j, g, 0], where).wait_recv()
            remote(vbuf.at[j, g], vbuf.at[j, g], kv_send.at[d, g, 1], kv_recv.at[j, g, 1], where).wait_recv()

        dtot[1] = dot32(skips[0], spread_mat[...]) + dot32(skips[1], spread_mat[...])
        def send_kv(g):
            for copy in own_kv(g):
                copy.wait()
            for d in range(1, ranks):
                @pl.when(c + d < ranks)
                def _():
                    for copy in kv_copies(d, g):
                        copy.start()

        def receive(i):
            at = pl.ds(pl.multiple_of(i * chunk, chunk), chunk)
            enter[:, at] = jnp.zeros((nstate, chunk), F32)
            for level in range(levels):
                @pl.when(lax.rem(c // 2 ** level, 2) == 1)
                def _():
                    state_copy(level, 0, i).wait_recv()
                    got = inbox[level, :, at].astype(F32)
                    if level > 0:
                        got = dvec[level, 0:1, at] * got
                    enter[:, at] = enter[:, at] + got

        forwards = (lax.rem(c, 2) == 1) & (c < ranks - 1)

        def onward(i):
            at = pl.ds(pl.multiple_of(i * chunk, chunk), chunk)
            return remote(mix_ref.at[0, :, at], stream.at[:, at], z_send.at[i], z_recv.at[i],
                          {"pipe": p + 1})

        lane = lax.broadcasted_iota(jnp.int32, (tokens, 2 * size), 1)

        def finish_mix(i, _):
            at = pl.ds(pl.multiple_of(i * chunk, chunk), chunk)

            receive(i)

            @pl.when(forwards)
            def _():
                outbox[:, at] = (dtot[0, 0:1, at] * enter[:, at] + local[:, at]).astype(BF16)
                for level in range(1, levels):
                    @pl.when(sends_at(level))
                    def _():
                        for d in range(2 ** level):
                            state_copy(level, d, i).start()

            @pl.when((lax.rem(c, 2) == 1) & (lax.rem(i, chunks // kv_heads) == 0))
            def _():
                send_kv(i // (chunks // kv_heads))

            mat = spread_mat[:, at]
            grown = dot32(since[0], mat) + dot32(since[1], mat)
            outer = grown * dot32(read_rows, enter[:, at].astype(BF16))
            outer = outer + dtot[1, 0:1, at] * x_ref[:, at].astype(F32)
            columns = cum_parts[i]
            lines = cum_rows[pl.ds(pl.multiple_of(i * chunk_heads, chunk_heads), chunk_heads), :]
            inner = []
            for k in range(0, chunk_heads, 2):
                both = []
                for h in (k, k + 1):
                    spread = jnp.minimum(columns[:, h:h + 1] - lines[h:h + 1, :], 0.0)
                    both.append((jnp.exp2(spread) * pair_mat[...]).astype(BF16))
                start = pl.multiple_of(i * chunk + k * size, 2 * size)
                xs = x_ref[:, pl.ds(start, 2 * size)]
                zero = jnp.zeros_like(xs)
                halves = jnp.concatenate(
                    [jnp.where(lane < size, xs, zero), jnp.where(lane < size, zero, xs)], axis=0)
                inner.append(dot32(jnp.concatenate(both, axis=1), halves))
            mix_ref[0, :, at] = (jnp.concatenate(inner, axis=1) + outer).astype(BF16)

            @pl.when(p < pipes - 1)
            def _():
                onward(i).start()
            return 0

        def make_local(i, _):
            at = pl.ds(pl.multiple_of(i * chunk, chunk), chunk)
            own_x(i).wait()
            mat = spread_mat[:, at]
            scaled = (dot32(tail[0], mat) + dot32(tail[1], mat)) * x_ref[:, at].astype(F32)
            state = dot32(write_ref[...], scaled.astype(BF16))
            local[:, at] = state

            @pl.when(lax.rem(c, 2) == 0)
            def _():
                outbox[:, at] = state.astype(BF16)
                state_copy(0, 0, i).start()

            @pl.when((lax.rem(c, 2) == 0) & (lax.rem(i, chunks // kv_heads) == 0))
            def _():
                send_kv(i // (chunks // kv_heads))

            @pl.when(c == 0)
            def _():
                finish_mix(i, 0)
            return 0

        lax.fori_loop(0, chunks, make_local, 0)

        for d in range(1, ranks):
            @pl.when(c >= d)
            def _():
                remote(tot_mine, tot_all.at[c - d], tt_send.at[d], tt_recv.at[c - d],
                       {"ctx": c}).wait_recv()
        def expand_row(logs):
            parts = split_two(jnp.exp2(logs)[:, :heads])
            return dot32(parts[0], spread_mat[...]) + dot32(parts[1], spread_mat[...])

        dtot[0] = expand_row(tot_mine[...])
        for level in range(1, levels):
            base = (c // 2 ** level) * 2 ** level
            logs = jnp.zeros((8, 128), F32)
            for j in range(ranks):
                logs = logs + jnp.where((j >= base) & (j < c), tot_all[j], 0.0)
            dvec[level] = expand_row(logs)

        for j in range(1, ranks):
            @pl.when(j > c)
            def _():
                kbuf[j] = jnp.zeros(kbuf.shape[1:], BF16)
                vbuf[j] = jnp.zeros(vbuf.shape[1:], BF16)
        bias[...] = jnp.where(
            lax.broadcasted_iota(jnp.int32, (tokens, keys), 1)
            <= c * tokens + lax.broadcasted_iota(jnp.int32, (tokens, keys), 0), 0.0, -1e30)
        q_copy.wait()

        def attend(i):
            g = i // (chunks // kv_heads)

            @pl.when(lax.rem(i, chunks // kv_heads) == 0)
            def _():
                for d in range(1, ranks):
                    @pl.when(c >= d)
                    def _():
                        wait_kv(d, g)
            kk = kbuf[:, g].reshape(keys, HEAD_DIM)
            vv = vbuf[:, g].reshape(keys, HEAD_DIM)
            for r in range(chunk // HEAD_DIM):
                at = pl.ds(pl.multiple_of(i * chunk + r * HEAD_DIM, HEAD_DIM), HEAD_DIM)
                s = lax.dot_general(q_ref[:, at], kk, (((1,), (1,)), ((), ())),
                                    preferred_element_type=F32)
                s = s * (LOG2E * HEAD_DIM ** -0.5) + bias[...]
                terms = jnp.exp2(s - jnp.max(s, axis=1, keepdims=True))
                weighted = dot32(terms.astype(BF16), vv)
                att[:, at] = weighted * (1.0 / jnp.sum(terms, axis=1, keepdims=True))

        def attend_one(i, _):
            attend(i)
            return 0

        lag = 1

        @pl.when(c > 0)
        def _():
            def main(i, _):
                @pl.when(i < chunks)
                def _():
                    finish_mix(i, 0)

                @pl.when(i >= lag)
                def _():
                    attend(i - lag)
                return 0
            lax.fori_loop(0, chunks + lag, main, 0)

        @pl.when(c == 0)
        def _():
            lax.fori_loop(0, chunks, attend_one, 0)

        @pl.when(p == 0)
        def _():
            in_copy.wait()

        sq_mine[...] = jnp.zeros_like(sq_mine)

        def add_up(i, _):
            at = pl.ds(pl.multiple_of(i * chunk, chunk), chunk)

            @pl.when(p > 0)
            def _():
                onward(i).wait_recv()
            summed = stream[:, at].astype(F32) + att[:, at]
            att[:, at] = summed
            square = summed * summed
            part = square[:, :128]
            for k in range(1, chunk // 128):
                part = part + square[:, k * 128:(k + 1) * 128]
            sq_mine[...] += part
            return 0

        lax.fori_loop(0, chunks, add_up, 0)
        swaps = [
            remote(sq_mine, sq_all.at[d - 1], e_send.at[d - 1], e_recv.at[d - 1],
                   {"exp": lax.rem(e + d, exps)})
            for d in range(1, exps)
        ]
        for copy in swaps:
            copy.start()
        for copy in swaps:
            copy.wait()
        squares = sq_mine[...]
        for d in range(exps - 1):
            squares = squares + sq_all[d]
        factor = lax.rsqrt(jnp.sum(squares, axis=1, keepdims=True) / D + 1e-05)

        def scale(i, _):
            at = pl.ds(pl.multiple_of(i * chunk, chunk), chunk)
            out_ref[0, :, at] = (att[:, at] * factor * gain_ref[0:1, at]).astype(BF16)
            return 0

        lax.fori_loop(0, chunks, scale, 0)

        for d in range(1, ranks):
            @pl.when(c + d < ranks)
            def _():
                tot_copy(d).wait_send()
                for g in range(kv_heads):
                    for copy in kv_copies(d, g):
                        copy.wait_send()
        for level in range(levels):
            @pl.when(sends_at(level))
            def _():
                def drain(i, _):
                    for d in range(2 ** level):
                        state_copy(level, d, i).wait_send()
                    return 0
                lax.fori_loop(0, chunks, drain, 0)

        @pl.when(p < pipes - 1)
        def _():
            def drain(i, _):
                onward(i).wait_send()
                return 0
            lax.fori_loop(0, chunks, drain, 0)

    scratch = [
        pltpu.VMEM((tokens, width), BF16),
        pltpu.VMEM((nstate, tokens), BF16),
        pltpu.VMEM((nstate, tokens), BF16),
        pltpu.VMEM((heads, tokens), F32),
        pltpu.VMEM((1, heads), F32),
        pltpu.VMEM((tokens, width), BF16),
        pltpu.VMEM((1, width), F32),
        pltpu.SemaphoreType.DMA((7,)),
        pltpu.SemaphoreType.DMA((chunks,)),
        pltpu.SemaphoreType.DMA((kv_heads, 2)),
        pltpu.VMEM((ranks, kv_heads, tokens, HEAD_DIM), BF16),
        pltpu.VMEM((ranks, kv_heads, tokens, HEAD_DIM), BF16),
        pltpu.VMEM((tokens, keys), F32),
        pltpu.VMEM((tokens, width), BF16),
        pltpu.VMEM((tokens, width), F32),
        pltpu.VMEM((nstate, width), F32),
        pltpu.VMEM((nstate, width), F32),
        pltpu.VMEM((nstate, width), BF16),
        pltpu.VMEM((levels, nstate, width), BF16),
        pltpu.VMEM((heads, width), BF16),
        pltpu.VMEM((chunks, tokens, 128), F32),
        pltpu.VMEM((128, tokens), F32),
        pltpu.VMEM((tokens, tokens), F32),
        pltpu.VMEM((2, 8, width), F32),
        pltpu.VMEM((levels, 8, width), F32),
        pltpu.VMEM((8, 128), F32),
        pltpu.VMEM((ranks, 8, 128), F32),
        pltpu.VMEM((tokens, 128), F32),
        pltpu.VMEM((max(exps - 1, 1), tokens, 128), F32),
        pltpu.SemaphoreType.DMA((ranks // 2, chunks)),
        pltpu.SemaphoreType.DMA((levels, chunks)),
        pltpu.SemaphoreType.DMA((ranks, kv_heads, 2)),
        pltpu.SemaphoreType.DMA((ranks, kv_heads, 2)),
        pltpu.SemaphoreType.DMA((ranks,)),
        pltpu.SemaphoreType.DMA((ranks,)),
        pltpu.SemaphoreType.DMA((chunks,)),
        pltpu.SemaphoreType.DMA((chunks,)),
        pltpu.SemaphoreType.DMA((exps,)),
        pltpu.SemaphoreType.DMA((exps,)),
    ]
    return kernel, scratch


def solution(mesh):
    pipes, ranks, exps = (mesh.shape[a] for a in ("pipe", "ctx", "exp"))

    def body(
        mix_input, state_write, state_read, log_decay, skip_gain, query_rows, key_rows,
        value_rows, incoming, norm_gain,
    ):
        tokens, width = mix_input.shape[1:]
        heads = skip_gain.shape[0]
        kernel, scratch = make_kernel(
            pipes, ranks, exps, tokens, heads, width, key_rows.shape[2], state_write.shape[2], 512)
        vmem = pl.BlockSpec(memory_space=pltpu.VMEM)
        shape = jax.ShapeDtypeStruct(mix_input.shape, BF16)
        return pl.pallas_call(
            kernel,
            out_shape=(shape, shape),
            in_specs=[pl.BlockSpec(memory_space=pltpu.HBM)] * 10,
            out_specs=(vmem, vmem),
            scratch_shapes=scratch,
            compiler_params=pltpu.CompilerParams(
                collective_id=0, has_side_effects=True, vmem_limit_bytes=60 * 2 ** 20),
        )(mix_input, jnp.swapaxes(state_write, 1, 2), jnp.swapaxes(state_read, 1, 2),
          jnp.swapaxes(log_decay, 1, 2), skip_gain[None], query_rows, key_rows,
          value_rows, incoming, norm_gain[None])

    placed = (
        P("pipe", "ctx", "exp"), P("pipe", "ctx", None), P("pipe", "ctx", None),
        P("pipe", "ctx", "exp"), P("exp"), P("pipe", "ctx", "exp"), P("pipe", "ctx", "exp"),
        P("pipe", "ctx", "exp"), P("ctx", "exp"), P("exp"),
    )
    return jax.shard_map(
        body, mesh=mesh, in_specs=placed,
        out_specs=(P("pipe", "ctx", "exp"), P("pipe", "ctx", "exp")), check_vma=False,
    )
```
